128 devices in a mesh: aux: 4 (over x_lo, core), ao: 32 (over z, y, x_hi).
Axes of the slice: x: 4 (x_hi: 2, x_lo: 2; x = x_hi * 2 + x_lo), y: 4, z: 4, core: 2. Of those that a mesh axis runs over, the one named last changes fastest.
Arguments:
- cholesky: bfloat16 [64, 4096, 4096], P('aux', 'ao'), may hold values from -3.5 to 3.5, as said below
- coeffs: bfloat16 [4096, 128], P('ao'), may hold values from -0.09375 to 0.09375
Outputs:
- integrals: float32 [16384, 16384], P('aux', 'ao')
The draws below stay inside these ranges and needn't reach their ends.
Inputs may be any that keep to these rules, and one draw needn't show every extreme that they name: cholesky[L, mu, nu] = cholesky[L, nu, mu] for every vector L.
All inputs are finite; a program needn't handle non-finite values.
Results may differ from the reference program's by a relative error of at most 0.0091.
Values may be sent and summed in bfloat16 or wider, within the bound.
No kernel may reach another device: no remote copies, remote signals or barrier semaphores. Data moves between devices by JAX's collectives and lax.ppermute only.
A program may use at most 64 MiB of HBM per device.

```python
import math
import jax
import jax.numpy as jnp
from jax import lax

NAO = 4096
NACT = 128
NVEC = 64


def draw_cholesky(key, part):
    slab_keys = jax.random.split(jax.random.fold_in(key, 11), NVEC)
    scales = jnp.ones((NVEC, NAO), jnp.float32)

    def one_slab(inputs):
        slab_key, row_scale = inputs
        values = 0.35 * jax.random.normal(slab_key, (NAO, NAO), jnp.float32)
        values = jnp.clip(values, -2.5, 2.5)
        sym = (values + values.T) / math.sqrt(2.0)
        sym = sym * row_scale[:, None] * row_scale[None, :]
        return jnp.clip(sym, -3.5, 3.5).astype(jnp.bfloat16)
    return lax.map(one_slab, (slab_keys, scales))


def steps_of(own_key, dims, cuts, smallest, high):
    loudness = 1.0
    for axis_at, shards_of in cuts:
        heights = jax.random.uniform(jax.random.fold_in(jax.random.fold_in(own_key, 6), axis_at), (shards_of,), jnp.float32, smallest / len(cuts), high / len(cuts))
        loudness = loudness * jnp.repeat(jnp.exp(heights), dims[axis_at] // shards_of).reshape((-1,) + (1,) * (len(dims) - 1 - axis_at))
    return loudness


def scatter_about(rng, extent, spread, bound, shards=(), held_as=jnp.bfloat16):
    drawn = jax.random.normal(rng, extent, jnp.float32) * spread
    if len(shards) > 0:
        drawn = steps_of(rng, extent, shards, -0.22, 0.18) * drawn
    return jnp.clip(drawn, min=-bound, max=bound).astype(held_as)


def setup_inputs(seed: int = 0) -> dict:
    seeds = jax.random.split(jax.random.key(seed), 3)
    cholesky = draw_cholesky(jax.random.fold_in(seeds[2], 71), 0)
    coeffs = scatter_about(seeds[1], (NAO, NACT), NAO ** -0.5, 0.09375, ((0, 32),))
    return {"cholesky": cholesky, "coeffs": coeffs}


def reference(cholesky, coeffs):
    def one_vector(slab):
        half = jnp.dot(slab, coeffs, preferred_element_type=jnp.float32).astype(jnp.bfloat16)
        return jnp.dot(coeffs.T, half, preferred_element_type=jnp.float32).astype(jnp.bfloat16)

    pairs = lax.map(one_vector, cholesky)
    flat_pairs = pairs.reshape(NVEC, NACT * NACT)
    return lax.dot_general(flat_pairs, flat_pairs, (((0,), (0,)), ((), ())), preferred_element_type=jnp.float32)
```

```python
import jax
import jax.numpy as jnp
from jax import lax
from jax.experimental import pallas as pl
from jax.experimental.pallas import tpu as pltpu
from jax.sharding import PartitionSpec as P

BF16, F32 = jnp.bfloat16, jnp.float32
VMEM = pl.BlockSpec(memory_space=pltpu.VMEM)
ANY = pl.BlockSpec(memory_space=pl.ANY)


def exchange(blocks, axes):
    return lax.all_to_all(blocks, axes, split_axis=0, concat_axis=0, tiled=True)


def start_window(chol_ref, held_ref, sem):
    span = held_ref.shape[2]
    wide = 2 * held_ref.shape[1]
    wides = chol_ref.shape[2] // wide
    at = lax.axis_index("ao") // 2

    def start(source, target, size):
        pltpu.make_async_copy(
            chol_ref.at[:, :, pl.ds(source, size)], held_ref.at[:, :, pl.ds(target, size)], sem
        ).start()

    for c in range(wides):

        @pl.when(at == c)
        def _(c=c):
            ahead = min(span, (wides - c) * wide)
            start(c * wide, 0, ahead)
            if ahead < span:
                start(0, ahead, span - ahead)


def wait_window(held_ref, sem):
    pltpu.make_async_copy(held_ref, held_ref, sem).wait()


def fetch(chol_ref, out_ref, sem):
    start_window(chol_ref.at[pl.ds(0, out_ref.shape[0])], out_ref, sem)
    wait_window(out_ref, sem)


def pair_sums(
    early_ref, chol_ref, mine_ref, other_ref, coeffs_ref, out_ref, held_ref, near_ref, sems, *, step
):
    ready, rows, span = early_ref.shape
    nvec = ready + held_ref.shape[0]
    blocks, part, active = mine_ref.shape
    wide = 2 * rows
    steps, wides = span // wide, blocks // 2
    core, at = lax.axis_index("aux") % 2, lax.axis_index("ao") // 2

    def late(first):
        return held_ref.at[pl.ds(first - ready, step)]

    for first in range(ready, nvec, step):
        start_window(chol_ref.at[pl.ds(first, step)], late(first), sems.at[first // step])
    for t in range(steps):
        for s in range(2):
            block = lax.rem(at + t, wides) * 2 + s
            for ref, half in ((mine_ref, core), (other_ref, 1 - core)):
                value = ref[block]
                if t in (0, steps - 1):
                    value = value * BF16(0.5)
                where = wide * t + rows * s + half * part
                near_ref[pl.ds(pl.multiple_of(where, part), part), :] = value
    near = near_ref[...]
    turned = coeffs_ref[...].astype(F32).T.astype(BF16)

    def finish(first, half):
        half = jnp.concatenate([half[v * rows : (v + 1) * rows] for v in range(step)], axis=1)
        sums = jnp.dot(turned, half, preferred_element_type=F32)
        for v in range(step):
            one = sums[:, v * active : (v + 1) * active]
            out_ref[first + v] = (one + one.T).astype(BF16)

    before = None
    for first in range(0, nvec, step):
        if first < ready:
            slab = early_ref[first : first + step]
        else:
            wait_window(late(first), sems.at[first // step])
            slab = late(first)[...]
        slab = slab.reshape(step * rows, span)
        half = jnp.dot(slab, near, preferred_element_type=F32).astype(BF16)
        if before is not None:
            finish(*before)
        before = first, half
    finish(*before)


def products(left_ref, right_ref, out_ref):
    auxes, count, deep, active = left_ref.shape
    nvec = right_ref.shape[0] // auxes
    for k in range(count):
        left = jnp.concatenate([left_ref[a, k, :nvec, :] for a in range(auxes)], axis=0)
        out_ref[k * active : (k + 1) * active, :] = lax.dot_general(
            left, right_ref[...], (((0,), (0,)), ((), ())), preferred_element_type=F32
        )


def on_device(cholesky, coeffs):
    nvec, rows, basis = cholesky.shape
    active = coeffs.shape[1]
    auxes, aos = lax.axis_size("aux"), lax.axis_size("ao")
    band, width = active // auxes, active // aos
    core = lax.axis_index("aux") % 2

    own = lax.dynamic_slice_in_dim(coeffs, core * (rows // 2), rows // 2, 0)
    mine = exchange(jnp.broadcast_to(own, (aos, rows // 2, active)), "ao")
    other = lax.ppermute(mine, "aux", [(a, a ^ 1) for a in range(auxes)])
    span, ready, step = (aos // 4 + 1) * 2 * rows, nvec // 2, 2
    early = pl.pallas_call(
        fetch,
        out_shape=jax.ShapeDtypeStruct((ready, rows, span), BF16),
        in_specs=[ANY],
        out_specs=VMEM,
        scratch_shapes=[pltpu.SemaphoreType.DMA(())],
        cost_estimate=pl.CostEstimate(
            flops=0, transcendentals=0, bytes_accessed=4 * ready * rows * span
        ),
        compiler_params=pltpu.CompilerParams(vmem_limit_bytes=44 << 20),
        name="fetch",
    )(cholesky)
    partial = pl.pallas_call(
        lambda *refs: pair_sums(*refs, step=step),
        out_shape=jax.ShapeDtypeStruct((nvec, active, active), BF16),
        in_specs=[VMEM, ANY, VMEM, VMEM, VMEM],
        out_specs=VMEM,
        scratch_shapes=[
            pltpu.VMEM((nvec - ready, rows, span), BF16),
            pltpu.VMEM((span, active), BF16),
            pltpu.SemaphoreType.DMA((nvec // step,)),
        ],
        compiler_params=pltpu.CompilerParams(vmem_limit_bytes=44 << 20),
        name="pair_sums",
    )(early, cholesky, mine, other, coeffs)

    partial = partial.reshape(nvec, auxes, aos, active)
    arrived = exchange(partial.transpose(2, 1, 0, 3), "ao")
    done = arrived.astype(F32).sum(axis=0).astype(BF16)

    left = jnp.broadcast_to(done[:, None], (auxes, aos, nvec, active))
    cols = done.reshape(auxes, nvec, aos, width).transpose(2, 0, 3, 1)
    cols = cols.reshape(1, aos, -1, active)
    cols = jnp.pad(cols, ((0, 0), (0, 0), (0, 8 - cols.shape[2]), (0, 0)))
    cols = jnp.broadcast_to(cols, (auxes, *cols.shape[1:]))
    sent = jnp.concatenate([left, cols], axis=2)
    got = exchange(sent.reshape(auxes * aos, nvec + 8, active), ("aux", "ao"))
    right = got[:, nvec:].reshape(auxes, aos, -1)[:, :, : auxes * width * nvec]
    right = right.reshape(auxes, aos, auxes, width, nvec).transpose(0, 4, 3, 2, 1)
    right = right.reshape(auxes * nvec, width * active)
    count = 8
    return pl.pallas_call(
        products,
        grid=(band // count,),
        out_shape=jax.ShapeDtypeStruct((band * active, width * active), F32),
        in_specs=[
            pl.BlockSpec((auxes, count, nvec + 8, active), lambda g: (0, g, 0, 0)),
            pl.BlockSpec((auxes * nvec, width * active), lambda g: (0, 0)),
        ],
        out_specs=pl.BlockSpec((count * active, width * active), lambda g: (g, 0)),
        compiler_params=pltpu.CompilerParams(vmem_limit_bytes=24 << 20),
        name="products",
    )(got.reshape(auxes, aos, nvec + 8, active), right)


def solution(mesh):
    in_specs = (P("aux", "ao", None), P("ao", None))
    out_specs = P("aux", "ao")
    return jax.shard_map(
        on_device, mesh=mesh, in_specs=in_specs, out_specs=out_specs, check_vma=False
    )
```

```python
import jax
import jax.numpy as jnp
from jax import lax
from jax.experimental import pallas as pl
from jax.experimental.pallas import tpu as pltpu
from jax.sharding import PartitionSpec as P

BF16, F32 = jnp.bfloat16, jnp.float32
VMEM = pl.BlockSpec(memory_space=pltpu.VMEM)
ANY = pl.BlockSpec(memory_space=pl.ANY)


def exchange(blocks, axes):
    return lax.all_to_all(blocks, axes, split_axis=0, concat_axis=0, tiled=True)


def start_window(chol_ref, held_ref, sem):
    span = held_ref.shape[2]
    wide = 2 * held_ref.shape[1]
    wides = chol_ref.shape[2] // wide
    at = lax.axis_index("ao") // 2

    def start(source, target, size):
        pltpu.make_async_copy(
            chol_ref.at[:, :, pl.ds(source, size)], held_ref.at[:, :, pl.ds(target, size)], sem
        ).start()

    for c in range(wides):

        @pl.when(at == c)
        def _(c=c):
            ahead = min(span, (wides - c) * wide)
            start(c * wide, 0, ahead)
            if ahead < span:
                start(0, ahead, span - ahead)


def wait_window(held_ref, sem):
    pltpu.make_async_copy(held_ref, held_ref, sem).wait()


def fetch(chol_ref, out_ref, sem):
    start_window(chol_ref.at[pl.ds(0, out_ref.shape[0])], out_ref, sem)
    wait_window(out_ref, sem)


def pair_sums(
    early_ref, chol_ref, mine_ref, other_ref, coeffs_ref, out_ref, held_ref, near_ref, sems, *, step, ahead
):
    ready, rows, span = early_ref.shape
    nvec = ready + held_ref.shape[0]
    blocks, part, active = mine_ref.shape
    wide = 2 * rows
    steps, wides = span // wide, blocks // 2
    core, at = lax.axis_index("aux") % 2, lax.axis_index("ao") // 2

    def late(first):
        return held_ref.at[pl.ds(first - ready, step)]

    def begin(first):
        if first < nvec:
            start_window(chol_ref.at[pl.ds(first, step)], late(first), sems.at[first // step])

    for first in range(ready, ready + ahead, step):
        begin(first)
    for t in range(steps):
        for s in range(2):
            block = lax.rem(at + t, wides) * 2 + s
            for ref, half in ((mine_ref, core), (other_ref, 1 - core)):
                value = ref[block]
                if t in (0, steps - 1):
                    value = value * BF16(0.5)
                where = wide * t + rows * s + half * part
                near_ref[pl.ds(pl.multiple_of(where, part), part), :] = value
    near = near_ref[...]
    turned = coeffs_ref[...].astype(F32).T.astype(BF16)

    def finish(first, half):
        half = jnp.concatenate([half[v * rows : (v + 1) * rows] for v in range(step)], axis=1)
        sums = jnp.dot(turned, half, preferred_element_type=F32)
        for v in range(step):
            one = sums[:, v * active : (v + 1) * active]
            out_ref[first + v] = (one + one.T).astype(BF16)

    before = None
    for first in range(0, nvec, step):
        if first < ready:
            slab = early_ref[first : first + step]
        else:
            wait_window(late(first), sems.at[first // step])
            begin(first + ahead)
            slab = late(first)[...]
        slab = slab.reshape(step * rows, span)
        half = jnp.dot(slab, near, preferred_element_type=F32).astype(BF16)
        if before is not None:
            finish(*before)
        before = first, half
    finish(*before)


def products(got_ref, out_ref, right_ref, held_ref, sems):
    auxes, aos, pieces, pair, active = got_ref.shape
    nvec = right_ref.shape[0] // auxes
    deep = nvec // pair
    width = right_ref.shape[1] // active
    part = width * nvec
    slots, size = held_ref.shape[:2]
    count = size // active

    for a in range(auxes):
        cols = []
        for piece in range(deep, pieces):
            both = got_ref[a, :, piece].astype(F32)
            for s in range(pair):
                row = both[:, s, :]
                cols += [row[:, c : c + part] for c in range(0, active, part)]
        turned = jnp.concatenate(cols, axis=0).T.astype(BF16)
        for v in range(width):
            right_ref[a * nvec : (a + 1) * nvec, v * active : (v + 1) * active] = turned[
                v * nvec : (v + 1) * nvec
            ]
    right = right_ref[...]

    def write(g):
        slot = g % slots
        return pltpu.make_async_copy(
            held_ref.at[slot], out_ref.at[pl.ds(g * size, size)], sems.at[slot]
        )

    groups = aos // count
    for g in range(groups):
        if g >= slots:
            write(g - slots).wait()
        for k in range(count):
            left = [got_ref[a, g * count + k, :deep].reshape(nvec, active) for a in range(auxes)]
            left = jnp.concatenate(left, axis=0)
            held_ref[g % slots, k * active : (k + 1) * active, :] = lax.dot_general(
                left, right, (((0,), (0,)), ((), ())), preferred_element_type=F32
            )
        write(g).start()
    for g in range(groups - slots, groups):
        write(g).wait()


def on_device(cholesky, coeffs):
    nvec, rows, basis = cholesky.shape
    active = coeffs.shape[1]
    auxes, aos = lax.axis_size("aux"), lax.axis_size("ao")
    band, width = active // auxes, active // aos
    core = lax.axis_index("aux") % 2

    own = lax.dynamic_slice_in_dim(coeffs, core * (rows // 2), rows // 2, 0)
    mine = exchange(jnp.broadcast_to(own, (aos, rows // 2, active)), "ao")
    other = lax.ppermute(mine, "aux", [(a, a ^ 1) for a in range(auxes)])
    span, ready, step, ahead = (aos // 4 + 1) * 2 * rows, 4, 2, 6
    early = pl.pallas_call(
        fetch,
        out_shape=jax.ShapeDtypeStruct((ready, rows, span), BF16),
        in_specs=[ANY],
        out_specs=VMEM,
        scratch_shapes=[pltpu.SemaphoreType.DMA(())],
        cost_estimate=pl.CostEstimate(
            flops=0, transcendentals=0, bytes_accessed=4 * ready * rows * span
        ),
        compiler_params=pltpu.CompilerParams(vmem_limit_bytes=44 << 20),
        name="fetch",
    )(cholesky)
    partial = pl.pallas_call(
        lambda *refs: pair_sums(*refs, step=step, ahead=ahead),
        out_shape=jax.ShapeDtypeStruct((nvec, active, active), BF16),
        in_specs=[VMEM, ANY, VMEM, VMEM, VMEM],
        out_specs=VMEM,
        scratch_shapes=[
            pltpu.VMEM((nvec - ready, rows, span), BF16),
            pltpu.VMEM((span, active), BF16),
            pltpu.SemaphoreType.DMA((nvec // step,)),
        ],
        compiler_params=pltpu.CompilerParams(vmem_limit_bytes=44 << 20),
        name="pair_sums",
    )(early, cholesky, mine, other, coeffs)

    partial = partial.reshape(nvec, auxes, aos, active)
    arrived = exchange(partial.transpose(2, 1, 0, 3), "ao")
    done = arrived.astype(F32).sum(axis=0).astype(BF16)

    extra = auxes * width * nvec // (2 * active)
    left = done.reshape(auxes, 1, nvec // 2, 2, active)
    left = jnp.pad(left, ((0, 0), (0, 0), (0, extra), (0, 0), (0, 0)))
    sent = jnp.broadcast_to(left, (auxes, aos, nvec // 2 + extra, 2, active))
    cols = done.reshape(auxes, nvec, aos, width).transpose(2, 0, 3, 1)
    cols = jnp.broadcast_to(
        cols.reshape(1, aos, extra, 2, active), (auxes, aos, extra, 2, active)
    )
    sent = lax.dynamic_update_slice(sent, cols, (0, 0, nvec // 2, 0, 0))
    got = exchange(sent.reshape(auxes * aos, nvec // 2 + extra, 2, active), ("aux", "ao"))
    got = got.reshape(auxes, aos, nvec // 2 + extra, 2, active)
    count, slots = 4, 4
    return pl.pallas_call(
        products,
        out_shape=jax.ShapeDtypeStruct((band * active, width * active), F32),
        in_specs=[VMEM],
        out_specs=ANY,
        scratch_shapes=[
            pltpu.VMEM((auxes * nvec, width * active), BF16),
            pltpu.VMEM((slots, count * active, width * active), F32),
            pltpu.SemaphoreType.DMA((slots,)),
        ],
        compiler_params=pltpu.CompilerParams(vmem_limit_bytes=24 << 20),
        name="products",
    )(got)


def solution(mesh):
    in_specs = (P("aux", "ao", None), P("ao", None))
    out_specs = P("aux", "ao")
    return jax.shard_map(
        on_device, mesh=mesh, in_specs=in_specs, out_specs=out_specs, check_vma=False
    )
```
